32 devices in a mesh: cuts: 2 (over x), mode: 16 (over z, y, core).
Axes of the slice: x: 2, y: 2, z: 4, core: 2. Of those that a mesh axis runs over, the one named last changes fastest.
Arguments:
- stem_tensor: float32 [2, 2, 16, 512, 512], P(None, 'cuts', 'mode'), parts along dimension 1, may hold values from -6 to 6
- branch_tensors: float32 [4, 2, 512, 512], replicated, may hold values from -0.1875 to 0.1875
- branch_order: int32 [4], replicated, may hold values from 0 to 3, each once
Outputs:
- new_stem: float32 [2, 2, 16, 512, 512], P(None, 'cuts', 'mode'), parts along dimension 1
The draws below stay inside these ranges and needn't reach their ends.
There are 2 independent parts, one for each index of `cuts`. The reference program is written for one: setup_inputs(seed, part) draws one part's arguments, and reference() takes and returns one part's arrays. A program takes and returns all parts, laid end to end along the dimension named above; an argument that names none is the same for every part. Nothing has to cross between parts.
Inputs may be any that keep to these rules, and one draw needn't show every extreme that they name: `branch_order`: a permutation of the 4 branch tensors.
All inputs are finite; a program needn't handle non-finite values.
Results may differ from the reference program's by a relative error of at most 0.00007.
Values sent between devices are 32-bit elements; how exact they have to be, the bound alone decides.
A program may use at most 64 MiB of HBM per device.

```python
import jax
import jax.numpy as jnp
from jax import lax

BW = 512
NB = 4
SL = 1
GRID = 16
N_MODE = 16


def level_of(stream_key, shape, shards, smallest, high):
    def one(position, parts):
        heights = jax.random.uniform(jax.random.fold_in(jax.random.fold_in(stream_key, 6), position), (parts,), jnp.float32, smallest / len(shards), high / len(shards))
        return jnp.repeat(jnp.exp(heights), shape[position] // parts).reshape((-1,) + (1,) * (len(shape) - position - 1))

    factor_of = one(*shards[0])
    for cut in shards[1:]:
        factor_of = factor_of * one(*cut)
    return factor_of


def noise(key, shape, scale, most, pieces=(), dtype=jnp.bfloat16):
    array = jax.random.normal(key, shape, jnp.float32) * scale
    if len(pieces) > 0:
        array = level_of(key, shape, pieces, -0.22, 0.18) * array
    return jnp.clip(array, min=-most, max=most).astype(dtype)


def setup_inputs(seed: int = 0, part: int = 0) -> dict:
    seeds = jax.random.split(jax.random.key(seed), 4)
    part_splits = jax.random.split(jax.random.fold_in(seeds[3], part), 4)
    stem_tensor = noise(part_splits[0], (2, SL, GRID, BW, BW), 1.0, 6.0, ((2, 16),), jnp.float32)
    branch_tensors = noise(seeds[1], (NB, 2, BW, BW), (2 * BW) ** -0.5, 0.1875, (), jnp.float32)
    branch_order = jax.random.permutation(seeds[2], NB).astype(jnp.int32)
    return dict(stem_tensor=stem_tensor, branch_tensors=branch_tensors, branch_order=branch_order)


def complex_product(first, second, form):
    high = lax.Precision.HIGHEST
    real = jnp.einsum(form, first[0], second[0], precision=high) - jnp.einsum(form, first[1], second[1], precision=high)
    imag = jnp.einsum(form, first[0], second[1], precision=high) + jnp.einsum(form, first[1], second[0], precision=high)
    return jnp.stack([real, imag])


def reference(stem_tensor, branch_tensors, branch_order):
    branches = [branch_tensors[branch_order[index]] for index in range(NB)]
    field = complex_product(stem_tensor, branches[0], 'sgce,cd->sgde')
    field = complex_product(field, branches[1], 'sgce,ed->sgcd')
    split = field.reshape(2, SL, N_MODE, N_MODE, BW // N_MODE, BW)
    split = jnp.swapaxes(split, 2, 3).reshape(2, SL, N_MODE, BW, BW)
    field = complex_product(split, branches[2], 'sgce,cd->sgde')
    return complex_product(field, branches[3], 'sgce,ed->sgcd')
```

```python
import functools

import jax
import jax.numpy as jnp
from jax import lax
from jax.experimental import pallas as pl
from jax.experimental.pallas import tpu as pltpu
from jax.sharding import PartitionSpec as P

MESH = pl.DeviceIdType.MESH
LANES = 128
F32, BF16 = jnp.float32, jnp.bfloat16


def flip(value, mask, size):
    result, bit = 0, 1
    while bit < size:
        digit = lax.rem(lax.div(value, bit), 2)
        result = result + (1 - digit if (mask // bit) % 2 else digit) * bit
        bit *= 2
    return result


def split(value):
    high = value.astype(BF16)
    return high, (value - high.astype(F32)).astype(BF16)


def dot(a, b):
    return jnp.dot(a, b, preferred_element_type=F32)


def dot3(high, low, right_high, right_low):
    return dot(high, right_high) + (dot(high, right_low) + dot(low, right_high))


def complex_rows(rows, right_high, right_low):
    m = rows.shape[0] // 2
    high, low = split(rows)
    by_real = dot3(high, low, right_high[0], right_low[0])
    by_imag = dot3(high, low, right_high[1], right_low[1])
    return by_real[:m] - by_imag[m:], by_imag[:m] + by_real[m:]


def kernel(n, order_ref, stem_ref, branch_ref, out_ref, stem, xh, xl, bh, bl, dh, dl, wh, wl,
           lch, lcl, sent, got, acc, load_sem, branch_sem, out_sem, send_sem, recv_sem, *branch):
    bw = stem.shape[1]
    rows = bw // n
    per = LANES // rows
    groups = n // per
    me = lax.axis_index("mode")
    z, q = lax.div(me, per), lax.rem(me, per)
    sequence = [groups // 2] + [s for s in range(1, groups) if s != groups // 2] + [0]
    early = sequence[: groups // 2]

    def column(s):
        return pl.ds(pl.multiple_of(flip(z, s, groups) * LANES, LANES), LANES)

    stem_copy = pltpu.make_async_copy(stem_ref, stem, load_sem)
    stem_copy.start()
    branch_copies = {}
    for s in sequence:
        branch_copies[s] = pltpu.make_async_copy(branch_ref.at[:, :, :, column(s)], branch[s], branch_sem.at[s])
        branch_copies[s].start()

    barrier = pltpu.get_barrier_semaphore()
    for k in range(1, n):
        pl.semaphore_signal(barrier, inc=1, device_id={"mode": flip(me, k, n)}, device_id_type=MESH)
    o0, o1, o2, o3 = (order_ref[k] for k in range(4))

    def first_rows(s):
        left = jnp.concatenate([branch[s][o0, part].T for part in range(2)], axis=0)
        return complex_rows(left, xh, xl)

    def hop(s, k):
        j = flip(q, k, per)
        return pltpu.make_async_remote_copy(
            src_ref=sent.at[s, j], dst_ref=got.at[s, q], send_sem=send_sem.at[s, k], recv_sem=recv_sem.at[s, q],
            device_id={"mode": flip(z, s, groups) * per + j}, device_id_type=MESH)

    def own(s):
        return pltpu.make_async_copy(sent.at[s, q], got.at[s, q], recv_sem.at[s, q])

    def send(s, real, imag):
        for j in range(per):
            sent[s, j, 0] = real[j * rows:(j + 1) * rows]
            sent[s, j, 1] = imag[j * rows:(j + 1) * rows]
        for k in range(per):
            own(s).start() if s == 0 and k == 0 else hop(s, k).start()

    stem_copy.wait()
    for part in range(2):
        xh[part], xl[part] = split(stem[part])
    for index, s in enumerate(sequence[: len(early)]):
        branch_copies[s].wait()
        real, imag = first_rows(s)
        if index == 0:
            pl.semaphore_wait(barrier, n - 1)
        send(s, real, imag)
    for s in sequence[len(early):]:
        branch_copies[s].wait()

    for s in range(groups):
        for part in range(2):
            bh[part, :, column(s)], bl[part, :, column(s)] = split(branch[s][o1, part])
            dh[part, :, column(s)], dl[part, :, column(s)] = split(branch[s][o3, part])

    def both(i, carry):
        at = pl.ds(pl.multiple_of(i * LANES, LANES), LANES)
        high = jnp.concatenate([bh[0, at], bh[1, at]], axis=0)
        low = jnp.concatenate([bl[0, at], bl[1, at]], axis=0)
        by_real = dot3(high, low, dh[0], dl[0])
        by_imag = dot3(high, low, dh[1], dl[1])
        wh[0, at], wl[0, at] = split(by_real[:LANES] - by_imag[LANES:])
        wh[1, at], wl[1, at] = split(by_imag[:LANES] + by_real[LANES:])
        return carry

    lax.fori_loop(0, bw // LANES, both, 0)

    for s in sequence[len(early):]:
        real, imag = first_rows(s)
        send(s, *complex_rows(jnp.concatenate([real, imag], axis=0), wh, wl))

    for s in range(groups):
        for t in range(groups):
            real, imag = (split(branch[t][o2, part, column(s), :].T) for part in range(2))
            top = column(t)
            low_half = pl.ds(pl.multiple_of(bw + flip(z, t, groups) * LANES, LANES), LANES)
            for ref, r, i in ((lch, real[0], imag[0]), (lcl, real[1], imag[1])):
                ref[s, top, :LANES] = r
                ref[s, top, LANES:] = -i
                ref[s, low_half, :LANES] = i
                ref[s, low_half, LANES:] = r

    arrivals = [0] + [s for s in early if s != groups // 2] + [groups // 2] + [s for s in sequence[len(early):] if s]
    tile = 2 * LANES
    for index, s in enumerate(arrivals):
        for j in range(per):
            pltpu.make_async_copy(got.at[s, j], got.at[s, j], recv_sem.at[s, j]).wait()
        real = jnp.concatenate([got[s, j, 0] for j in range(per)], axis=0)
        imag = jnp.concatenate([got[s, j, 1] for j in range(per)], axis=0)
        arrived = jnp.concatenate([real, imag], axis=0)
        if s in early:
            arrived = jnp.concatenate(complex_rows(arrived, wh, wl), axis=0)
        right_high, right_low = split(arrived)
        for i in range(2 * bw // tile):
            at = slice(i * tile, (i + 1) * tile)
            add = dot3(lch[s, at], lcl[s, at], right_high, right_low)
            acc[at] = add if index == 0 else acc[at] + add
            if index == len(arrivals) - 1:
                part, row = divmod(i * tile, bw)
                pltpu.make_async_copy(acc.at[at], out_ref.at[part, pl.ds(row, tile)], out_sem.at[i]).start()
    for i in range(2 * bw // tile):
        part, row = divmod(i * tile, bw)
        pltpu.make_async_copy(acc.at[pl.ds(i * tile, tile)], out_ref.at[part, pl.ds(row, tile)], out_sem.at[i]).wait()
    for s in range(groups):
        for k in range(per):
            if s or k:
                hop(s, k).wait_send()


def fused(n, stem_tensor, branch_tensors, branch_order):
    bw = stem_tensor.shape[-1]
    rows = bw // n
    per = LANES // rows
    groups = n // per
    square = pltpu.VMEM((2, bw, bw), BF16)
    window = pltpu.VMEM((groups, 2 * bw, 2 * LANES), BF16)
    return pl.pallas_call(
        functools.partial(kernel, n),
        out_shape=jax.ShapeDtypeStruct((2, bw, bw), F32),
        in_specs=[pl.BlockSpec(memory_space=pltpu.SMEM)] + [pl.BlockSpec(memory_space=pl.ANY)] * 2,
        out_specs=pl.BlockSpec(memory_space=pl.ANY),
        scratch_shapes=[
            pltpu.VMEM((2, bw, bw), F32),
            *[square] * 8,
            window,
            window,
            pltpu.VMEM((groups, per, 2, rows, bw), F32),
            pltpu.VMEM((groups, per, 2, rows, bw), F32),
            pltpu.VMEM((2 * bw, bw), F32),
            pltpu.SemaphoreType.DMA,
            pltpu.SemaphoreType.DMA((groups,)),
            pltpu.SemaphoreType.DMA((bw // LANES,)),
            pltpu.SemaphoreType.DMA((groups, per)),
            pltpu.SemaphoreType.DMA((groups, per)),
            *[pltpu.VMEM((4, 2, bw, LANES), F32)] * groups,
        ],
        compiler_params=pltpu.CompilerParams(collective_id=0, has_side_effects=True, vmem_limit_bytes=56 << 20),
    )(branch_order, stem_tensor.reshape(2, bw, bw), branch_tensors).reshape(stem_tensor.shape)


def complex_product(first, second, form):
    high = lax.Precision.HIGHEST
    real = jnp.einsum(form, first[0], second[0], precision=high) - jnp.einsum(form, first[1], second[1], precision=high)
    imag = jnp.einsum(form, first[0], second[1], precision=high) + jnp.einsum(form, first[1], second[0], precision=high)
    return jnp.stack([real, imag])


def plain(stem_tensor, branch_tensors, branch_order):
    field = stem_tensor[:, :, 0]
    chosen = [branch_tensors[branch_order[index]] for index in range(4)]
    field = complex_product(field, chosen[0], "sce,cd->sde")
    field = complex_product(field, chosen[1], "sce,ed->scd")
    moved = lax.all_to_all(field[:, :, None], "mode", split_axis=3, concat_axis=2, tiled=True)
    merged = moved.reshape(field.shape)
    merged = complex_product(merged, chosen[2], "sce,cd->sde")
    return complex_product(merged, chosen[3], "sce,ed->scd")[:, :, None]


def on_device(n, stem_tensor, branch_tensors, branch_order):
    _, stems, held, bw, _ = stem_tensor.shape
    rows = bw // n
    fits = stems == held == 1 and rows % 8 == 0 and rows < LANES and n & (n - 1) == 0 and n * rows == bw
    if fits and bw % (2 * LANES) == 0:
        return fused(n, stem_tensor, branch_tensors, branch_order)
    return plain(stem_tensor, branch_tensors, branch_order)


def solution(mesh):
    return jax.shard_map(
        functools.partial(on_device, mesh.shape["mode"]),
        mesh=mesh,
        in_specs=(P(None, "cuts", "mode", None, None), P(), P()),
        out_specs=P(None, "cuts", "mode", None, None),
        check_vma=False,
    )
```

```python
import functools

import jax
import jax.numpy as jnp
from jax import lax
from jax.experimental import pallas as pl
from jax.experimental.pallas import tpu as pltpu
from jax.sharding import PartitionSpec as P

MESH = pl.DeviceIdType.MESH
LANES = 128
F32, BF16 = jnp.float32, jnp.bfloat16


def flip(value, mask, size):
    result, bit = 0, 1
    while bit < size:
        digit = lax.rem(lax.div(value, bit), 2)
        result = result + (1 - digit if (mask // bit) % 2 else digit) * bit
        bit *= 2
    return result


def split(value):
    high = value.astype(BF16)
    return high, (value - high.astype(F32)).astype(BF16)


def dot(a, b):
    return jnp.dot(a, b, preferred_element_type=F32)


def dot3(high, low, right_high, right_low):
    return dot(high, right_high) + (dot(high, right_low) + dot(low, right_high))


def complex_rows(rows, right_high, right_low):
    m = rows.shape[0] // 2
    high, low = split(rows)
    by_real = dot3(high, low, right_high[0], right_low[0])
    by_imag = dot3(high, low, right_high[1], right_low[1])
    return by_real[:m] - by_imag[m:], by_imag[:m] + by_real[m:]


def kernel(n, order_ref, stem_ref, branch_ref, out_ref, stem, xh, xl, bh, bl, dh, dl, wh, wl,
           lch, lcl, lct, sent, got, acc, load_sem, branch_sem, out_sem, send_sem, recv_sem, *branch):
    bw = stem.shape[1]
    rows = bw // n
    per = LANES // rows
    groups = n // per
    me = lax.axis_index("mode")
    z, q = lax.div(me, per), lax.rem(me, per)
    sequence = [groups // 2] + [s for s in range(1, groups) if s != groups // 2] + [0]
    early = sequence[: groups // 2]

    def column(s):
        return pl.ds(pl.multiple_of(flip(z, s, groups) * LANES, LANES), LANES)

    stem_copies = [pltpu.make_async_copy(stem_ref.at[part], stem.at[part], load_sem.at[part]) for part in range(2)]
    branch_copies = {}
    for s in sequence:
        branch_copies[s] = pltpu.make_async_copy(branch_ref.at[:, :, :, column(s)], branch[s], branch_sem.at[s])
        if s == sequence[0]:
            branch_copies[s].start()
    for copy in stem_copies:
        copy.start()

    barrier = pltpu.get_barrier_semaphore()
    for k in range(1, n):
        pl.semaphore_signal(barrier, inc=1, device_id={"mode": flip(me, k, n)}, device_id_type=MESH)
    o0, o1, o2, o3 = (order_ref[k] for k in range(4))

    def left_rows(s):
        return jnp.concatenate([branch[s][o0, part].T for part in range(2)], axis=0)

    def first_rows(s):
        return complex_rows(left_rows(s), xh, xl)

    def hop(s, k):
        j = flip(q, k, per)
        return pltpu.make_async_remote_copy(
            src_ref=sent.at[s, j], dst_ref=got.at[s, q], send_sem=send_sem.at[s, k], recv_sem=recv_sem.at[s, q],
            device_id={"mode": flip(z, s, groups) * per + j}, device_id_type=MESH)

    def own(s):
        return pltpu.make_async_copy(sent.at[s, q], got.at[s, q], recv_sem.at[s, q])

    def send(s, real, imag):
        for j in range(per):
            sent[s, j, 0] = real[j * rows:(j + 1) * rows]
            sent[s, j, 1] = imag[j * rows:(j + 1) * rows]
        for k in range(per):
            own(s).start() if s == 0 and k == 0 else hop(s, k).start()

    branch_copies[sequence[0]].wait()
    high, low = split(left_rows(sequence[0]))
    by = []
    for part in range(2):
        stem_copies[part].wait()
        if part == 1:
            for s in sequence[1:]:
                branch_copies[s].start()
        xh[part], xl[part] = split(stem[part])
        by.append(dot3(high, low, xh[part], xl[part]))
    real, imag = by[0][:LANES] - by[1][LANES:], by[1][:LANES] + by[0][LANES:]
    pl.semaphore_wait(barrier, n - 1)
    send(sequence[0], real, imag)
    for s in early[1:]:
        branch_copies[s].wait()
        send(s, *first_rows(s))
    for s in sequence[len(early):]:
        branch_copies[s].wait()

    for s in range(groups):
        for part in range(2):
            bh[part, :, column(s)], bl[part, :, column(s)] = split(branch[s][o1, part])
            dh[part, :, column(s)], dl[part, :, column(s)] = split(branch[s][o3, part])

    def both(i, carry):
        at = pl.ds(pl.multiple_of(i * LANES, LANES), LANES)
        high = jnp.concatenate([bh[0, at], bh[1, at]], axis=0)
        low = jnp.concatenate([bl[0, at], bl[1, at]], axis=0)
        by_real = dot3(high, low, dh[0], dl[0])
        by_imag = dot3(high, low, dh[1], dl[1])
        wh[0, at], wl[0, at] = split(by_real[:LANES] - by_imag[LANES:])
        wh[1, at], wl[1, at] = split(by_imag[:LANES] + by_real[LANES:])
        return carry

    lax.fori_loop(0, bw // LANES, both, 0)

    for s in sequence[len(early):]:
        real, imag = first_rows(s)
        send(s, *complex_rows(jnp.concatenate([real, imag], axis=0), wh, wl))

    last = sequence[-2]

    def third_rows(t, part, s):
        if s != last:
            return branch[t][o2, part, column(s), :]
        base = flip(z, s, groups) * LANES
        return jnp.concatenate([
            branch[t][o2, part, pl.ds(pl.multiple_of(base + flip(q, k, per) * rows, rows), rows), :]
            for k in range(per)], axis=0)

    for s in range(groups):
        for t in range(groups):
            real, imag = (split(third_rows(t, part, s).T) for part in range(2))
            top = column(t)
            low_half = pl.ds(pl.multiple_of(bw + flip(z, t, groups) * LANES, LANES), LANES)
            for ref, r, i in ((lch, real[0], imag[0]), (lcl, real[1], imag[1])):
                ref[s, top, :LANES] = r
                ref[s, top, LANES:] = -i
                ref[s, low_half, :LANES] = i
                ref[s, low_half, LANES:] = r
            if s == last:
                tail = slice(LANES - rows, LANES)
                for place, (r, i) in enumerate(((real[0], imag[0]), (real[0], imag[0]), (real[1], imag[1]))):
                    at = slice(2 * place * rows, (2 * place + 1) * rows)
                    after = slice((2 * place + 1) * rows, (2 * place + 2) * rows)
                    lct[top, at] = r[:, tail]
                    lct[top, after] = -i[:, tail]
                    lct[low_half, at] = i[:, tail]
                    lct[low_half, after] = r[:, tail]

    arrivals = [0] + [s for s in early if s != groups // 2] + [groups // 2] + [s for s in sequence[len(early):] if s]
    tile = 2 * LANES

    def arrive(s, j):
        pltpu.make_async_copy(got.at[s, j], got.at[s, j], recv_sem.at[s, j]).wait()

    for index, s in enumerate(arrivals):
        places = [flip(q, k, per) if s == last else k for k in range(per)]
        if s == last:
            final = places.pop()
        for j in places:
            arrive(s, j)
        blank = [jnp.zeros((rows, bw), F32)] * (per - len(places))
        arrived = jnp.concatenate([piece for part in range(2) for piece in [got[s, j, part] for j in places] + blank], axis=0)
        if s in early:
            arrived = jnp.concatenate(complex_rows(arrived, wh, wl), axis=0)
        right_high, right_low = split(arrived)
        for i in range(2 * bw // tile):
            at = slice(i * tile, (i + 1) * tile)
            add = dot3(lch[s, at], lcl[s, at], right_high, right_low)
            acc[at] = add if index == 0 else acc[at] + add
    arrive(last, final)
    high, low = split(jnp.concatenate([got[last, final, 0], got[last, final, 1]], axis=0))
    right = jnp.concatenate([high, low, high], axis=0)
    for i in range(2 * bw // tile):
        at = slice(i * tile, (i + 1) * tile)
        acc[at] = acc[at] + dot(lct[at, : 6 * rows], right)
        part, row = divmod(i * tile, bw)
        pltpu.make_async_copy(acc.at[at], out_ref.at[part, pl.ds(row, tile)], out_sem.at[i]).start()
    for i in range(2 * bw // tile):
        part, row = divmod(i * tile, bw)
        pltpu.make_async_copy(acc.at[pl.ds(i * tile, tile)], out_ref.at[part, pl.ds(row, tile)], out_sem.at[i]).wait()
    for s in range(groups):
        for k in range(per):
            if s or k:
                hop(s, k).wait_send()


def fused(n, stem_tensor, branch_tensors, branch_order):
    bw = stem_tensor.shape[-1]
    rows = bw // n
    per = LANES // rows
    groups = n // per
    square = pltpu.VMEM((2, bw, bw), BF16)
    hbm = functools.partial(pltpu.with_memory_space_constraint, memory_space=pltpu.HBM)
    window = pltpu.VMEM((groups, 2 * bw, 2 * LANES), BF16)
    return pl.pallas_call(
        functools.partial(kernel, n),
        out_shape=jax.ShapeDtypeStruct((2, bw, bw), F32),
        in_specs=[pl.BlockSpec(memory_space=pltpu.SMEM)] + [pl.BlockSpec(memory_space=pl.ANY)] * 2,
        out_specs=pl.BlockSpec(memory_space=pl.ANY),
        scratch_shapes=[
            pltpu.VMEM((2, bw, bw), F32),
            *[square] * 8,
            window,
            window,
            pltpu.VMEM((2 * bw, 2 * LANES), BF16),
            pltpu.VMEM((groups, per, 2, rows, bw), F32),
            pltpu.VMEM((groups, per, 2, rows, bw), F32),
            pltpu.VMEM((2 * bw, bw), F32),
            pltpu.SemaphoreType.DMA((2,)),
            pltpu.SemaphoreType.DMA((groups,)),
            pltpu.SemaphoreType.DMA((bw // LANES,)),
            pltpu.SemaphoreType.DMA((groups, per)),
            pltpu.SemaphoreType.DMA((groups, per)),
            *[pltpu.VMEM((4, 2, bw, LANES), F32)] * groups,
        ],
        compiler_params=pltpu.CompilerParams(collective_id=0, has_side_effects=True, vmem_limit_bytes=32 << 20),
    )(hbm(branch_order), hbm(stem_tensor.reshape(2, bw, bw)), hbm(branch_tensors)).reshape(stem_tensor.shape)


def complex_product(first, second, form):
    high = lax.Precision.HIGHEST
    real = jnp.einsum(form, first[0], second[0], precision=high) - jnp.einsum(form, first[1], second[1], precision=high)
    imag = jnp.einsum(form, first[0], second[1], precision=high) + jnp.einsum(form, first[1], second[0], precision=high)
    return jnp.stack([real, imag])


def plain(stem_tensor, branch_tensors, branch_order):
    field = stem_tensor[:, :, 0]
    chosen = [branch_tensors[branch_order[index]] for index in range(4)]
    field = complex_product(field, chosen[0], "sce,cd->sde")
    field = complex_product(field, chosen[1], "sce,ed->scd")
    moved = lax.all_to_all(field[:, :, None], "mode", split_axis=3, concat_axis=2, tiled=True)
    merged = moved.reshape(field.shape)
    merged = complex_product(merged, chosen[2], "sce,cd->sde")
    return complex_product(merged, chosen[3], "sce,ed->scd")[:, :, None]


def on_device(n, stem_tensor, branch_tensors, branch_order):
    _, stems, held, bw, _ = stem_tensor.shape
    rows = bw // n
    fits = stems == held == 1 and rows % 8 == 0 and 3 * rows <= LANES and n & (n - 1) == 0 and n * rows == bw
    if fits and bw % (4 * LANES) == 0:
        return fused(n, stem_tensor, branch_tensors, branch_order)
    return plain(stem_tensor, branch_tensors, branch_order)


def solution(mesh):
    return jax.shard_map(
        functools.partial(on_device, mesh.shape["mode"]),
        mesh=mesh,
        in_specs=(P(None, "cuts", "mode", None, None), P(), P()),
        out_specs=P(None, "cuts", "mode", None, None),
        check_vma=False,
    )
```
